32 devices in a mesh: gx: 8 (over z, core), gy: 4 (over y, x).
Axes of the slice: x: 2, y: 2, z: 4, core: 2. Of those that a mesh axis runs over, the one named last changes fastest.
Arguments:
- grid_field: bfloat16 [1, 20, 2048, 2048], P(None, None, 'gx', 'gy'), may hold values from -8 to 8
- spectral_weight: float32 [2, 2, 20, 20, 2048], P(None, None, None, None, ('gx', 'gy')), may hold values from -1 to 1
- conv_near: bfloat16 [2, 20, 180], replicated, may hold values from -0.4375 to 0.4375
- conv_far: bfloat16 [2, 20, 500], replicated, may hold values from -0.25 to 0.25
- mix_logits: float32 [2, 3], replicated, may hold values from -1 to 1
- channel_bias: float32 [2, 20], replicated, may hold values from -3 to 3
Outputs:
- result_field: bfloat16 [1, 20, 2048, 2048], P(None, None, 'gx', 'gy')
The draws below stay inside these ranges and needn't reach their ends.
All inputs are finite; a program needn't handle non-finite values.
Results may differ from the reference program's by a relative error of at most 0.004.
Values may be sent and summed in bfloat16 or wider, within the bound.
A program may use at most 448 MiB of HBM per device.

```python
import math
import jax
import jax.numpy as jnp
from jax import lax

NX = 2048
NY = 2048
C = 20
MX = 32
MY = 32
LAYERS = 2
PLANES = 1
KX = 64
MODES = 2048


def wave_profile(sub_key, length, highest_mode):
    sub_keys = jax.random.split(sub_key, 2)
    frequency = jnp.arange(highest_mode, dtype=jnp.int32)
    amplitude = jax.random.normal(sub_keys[0], (PLANES, C, highest_mode, 1), jnp.float32) * math.sqrt(2.0 / highest_mode)
    phases = jax.random.uniform(sub_keys[1], (PLANES, C, highest_mode, 1), jnp.float32, 0.0, 2.0 * math.pi)
    positions = jnp.arange(length, dtype=jnp.int32)
    angle_grid = (frequency[:, None] * positions[None, :] % length).astype(jnp.float32) * (2.0 * math.pi / length)
    return jnp.sum(amplitude * jnp.cos(angle_grid[None, None, :, :] + phases), axis=2)


def draw_grid_field(key, part):
    noise_key, first_key, second_key = jax.random.split(jax.random.fold_in(key, 17), 3)
    roughness = jax.random.normal(noise_key, (PLANES, C, NX, NY), jnp.float32)
    profile_rows = wave_profile(first_key, NX, MX)
    profile_cols = wave_profile(second_key, NY, MY)
    smooth = profile_rows[:, :, :, None] * profile_cols[:, :, None, :]
    return jnp.clip(roughness + smooth, -8.0, 8.0).astype(jnp.bfloat16)


def level_of(stream_key, shape, cuts, low, largest):
    factor_of = 1.0
    for dim, shards_of in cuts:
        steps = jax.random.uniform(jax.random.fold_in(jax.random.fold_in(stream_key, 6), dim), (shards_of,), jnp.float32, low / len(cuts), largest / len(cuts))
        factor_of = factor_of * jnp.repeat(jnp.exp(steps), shape[dim] // shards_of).reshape((-1,) + (1,) * (len(shape) - 1 - dim))
    return factor_of


def scatter_about(rng, extent, deviation, reach, pieces=(), kind=jnp.bfloat16):
    values = jax.random.normal(rng, extent, jnp.float32) * deviation
    if len(pieces) > 0:
        values = level_of(rng, extent, pieces, -0.22, 0.18) * values
    return jnp.clip(values, min=-reach, max=reach).astype(kind)


def setup_inputs(seed: int = 0) -> dict:
    streams_of = jax.random.split(jax.random.key(seed), 7)
    grid_field = draw_grid_field(jax.random.fold_in(streams_of[6], 71), 0)
    spectral_weight = scatter_about(streams_of[1], (LAYERS, 2, C, C, MODES), (2 * C) ** -0.5, 1.0, ((4, 32),), jnp.float32)
    conv_near = scatter_about(streams_of[2], (LAYERS, C, 9 * C), (9 * C) ** -0.5, 0.4375)
    conv_far = scatter_about(streams_of[3], (LAYERS, C, 25 * C), (25 * C) ** -0.5, 0.25)
    mix_logits = jnp.clip(jax.random.uniform(streams_of[4], (LAYERS, 3), jnp.float32, -1.0, 1.0), -1.0, 1.0)
    channel_bias = scatter_about(streams_of[5], (LAYERS, C), 0.5, 3.0, (), jnp.float32)
    return {"grid_field": grid_field, "spectral_weight": spectral_weight, "conv_near": conv_near, "conv_far": conv_far, "mix_logits": mix_logits, "channel_bias": channel_bias}


full_turn = 2.0 * math.pi
highest = lax.Precision.HIGHEST


def forward_table(positions):
    col_modes = jnp.arange(MY, dtype=jnp.int32)
    phases = ((positions[:, None] * col_modes[None, :]) % NY).astype(jnp.float32) * (full_turn / NY)
    return jnp.concatenate([jnp.cos(phases), -jnp.sin(phases)], axis=1).astype(jnp.bfloat16)


def row_tables(positions):
    lower = jnp.arange(MX, dtype=jnp.int32)
    row_modes = jnp.concatenate([lower, lower + (NX - MX)])
    phases = ((positions[:, None] * row_modes[None, :]) % NX).astype(jnp.float32) * (full_turn / NX)
    return jnp.cos(phases), jnp.sin(phases)


def inverse_table(positions):
    col_modes = jnp.arange(MY, dtype=jnp.int32)
    col_weight = jnp.where(col_modes == 0, 1.0, 2.0).astype(jnp.float32) / (NX * NY)
    phases = ((col_modes[:, None] * positions[None, :]) % NY).astype(jnp.float32) * (full_turn / NY)
    return jnp.concatenate([jnp.cos(phases) * col_weight[:, None], -jnp.sin(phases) * col_weight[:, None]], axis=0)


def block_height():
    height = min(NX, 128)
    while NX % height != 0:
        height = height - 1
    return height


def mixed_spectrum(plane_field, weight_pair, forward_cols, cosine_rows, sine_rows):
    channels = plane_field.shape[0]
    line_sums = jnp.dot(plane_field.reshape(channels * NX, NY), forward_cols, preferred_element_type=jnp.float32)
    line_sums = line_sums.reshape(channels, NX, 2 * MY)
    real_lines = line_sums[..., :MY]
    imaginary_lines = line_sums[..., MY:]

    def contract_rows(operand, lookup):
        return jnp.einsum("cxk,xj->cjk", operand, lookup, precision=highest)

    real_spec = (contract_rows(real_lines, cosine_rows) + contract_rows(imaginary_lines, sine_rows)).reshape(channels, MODES)
    imaginary_spec = (contract_rows(imaginary_lines, cosine_rows) - contract_rows(real_lines, sine_rows)).reshape(channels, MODES)

    def mix_modes(spectrum, weights):
        return jnp.einsum("cm,com->om", spectrum, weights, precision=highest)

    real_mixed = mix_modes(real_spec, weight_pair[0]) - mix_modes(imaginary_spec, weight_pair[1])
    imaginary_mixed = mix_modes(imaginary_spec, weight_pair[0]) + mix_modes(real_spec, weight_pair[1])
    return real_mixed.reshape(channels, KX, MY), imaginary_mixed.reshape(channels, KX, MY)


def conv_block(padded_rows, tap_weights, dilation, side_taps, height):
    channels = padded_rows.shape[0]
    accumulated = jnp.zeros((channels, height * NY), jnp.float32)
    for tap_index in range(side_taps * side_taps):
        shift_row = (tap_index // side_taps - side_taps // 2) * dilation
        shift_col = (tap_index % side_taps - side_taps // 2) * dilation
        piece = padded_rows[:, 4 + shift_row:4 + shift_row + height, 4 + shift_col:4 + shift_col + NY]
        piece = piece.astype(jnp.float32).reshape(channels, height * NY)
        weights_tap = tap_weights[:, tap_index * channels:(tap_index + 1) * channels].astype(jnp.float32)
        accumulated = accumulated + jnp.dot(weights_tap, piece, precision=highest)
    return accumulated.reshape(channels, height, NY)


def reference(grid_field, spectral_weight, conv_near, conv_far, mix_logits, channel_bias):
    row_positions = jnp.arange(NX, dtype=jnp.int32)
    col_positions = jnp.arange(NY, dtype=jnp.int32)
    cosine_rows, sine_rows = row_tables(row_positions)
    forward_cols = forward_table(col_positions)
    inverse_cols = inverse_table(col_positions)
    height = block_height()
    block_starts = jnp.arange(NX // height, dtype=jnp.int32) * height

    def per_plane(plane_field):
        channels = plane_field.shape[0]
        for layer_index in range(LAYERS):
            real_mixed, imaginary_mixed = mixed_spectrum(plane_field, spectral_weight[layer_index], forward_cols, cosine_rows, sine_rows)
            padded = jnp.pad(plane_field, ((0, 0), (4, 4), (4, 4)), mode="wrap")
            exponents = jnp.exp(mix_logits[layer_index])
            mixture = exponents / jnp.sum(exponents)
            bias_column = channel_bias[layer_index][:, None, None]
            near_weights = conv_near[layer_index]
            far_weights = conv_far[layer_index]

            def per_block(start):
                cos_block = lax.dynamic_slice_in_dim(cosine_rows, start, height, 0)
                sin_block = lax.dynamic_slice_in_dim(sine_rows, start, height, 0)

                def expand_rows(spectrum, lookup):
                    return jnp.einsum("cjk,xj->cxk", spectrum, lookup, precision=highest)

                real_rows = expand_rows(real_mixed, cos_block) - expand_rows(imaginary_mixed, sin_block)
                imaginary_rows = expand_rows(real_mixed, sin_block) + expand_rows(imaginary_mixed, cos_block)
                stacked = jnp.concatenate([real_rows, imaginary_rows], axis=-1).reshape(channels * height, 2 * MY)
                spectral = jnp.dot(stacked, inverse_cols, precision=highest).reshape(channels, height, NY)
                padded_rows = lax.dynamic_slice_in_dim(padded, start, height + 8, 1)
                near_term = conv_block(padded_rows, near_weights, 1, 3, height)
                far_term = conv_block(padded_rows, far_weights, 2, 5, height)
                summed = mixture[0] * spectral + mixture[1] * near_term + mixture[2] * far_term + bias_column
                return jax.nn.gelu(summed, approximate=False).astype(jnp.bfloat16)

            blocks = lax.map(per_block, block_starts)
            plane_field = jnp.transpose(blocks, (1, 0, 2, 3)).reshape(channels, NX, NY)
        return plane_field

    return lax.map(per_plane, grid_field)
```

```python
import math

import jax
import jax.numpy as jnp
from jax import lax
from jax.experimental import pallas as pl
from jax.experimental.pallas import tpu as pltpu
from jax.sharding import PartitionSpec as P

full_turn = 2.0 * math.pi
highest = lax.Precision.HIGHEST
HALO = 4
GROUP = 16
SUB = 8
SLAB = SUB + 2 * HALO


def padded_field(value):
    for axis, dim in (("gx", 1), ("gy", 2)):
        size, length = (lax.axis_size(axis), value.shape[dim])
        up = [(i, (i + 1) % size) for i in range(size)]
        down = [(j, i) for i, j in up]
        last = lax.slice_in_dim(value, length - HALO, length, axis=dim)
        first = lax.slice_in_dim(value, 0, HALO, axis=dim)
        before = lax.ppermute(last, axis, up)
        after = lax.ppermute(first, axis, down)
        pieces = [before, value, after]
        if dim == 1:
            tail = value.shape[:1] + (GROUP - 2 * HALO,) + value.shape[2:]
            pieces.append(jnp.zeros(tail, value.dtype))
        value = jnp.concatenate(pieces, axis=dim)
    return value


def mode_numbers(modes_x, modes_y, cells_x):
    half = modes_x // 2
    lower = jnp.arange(half, dtype=jnp.int32)
    return jnp.concatenate([lower, lower + (cells_x - half)]), jnp.arange(modes_y, dtype=jnp.int32)


def slab_weights(taps, dilation, side):
    channels = taps.shape[0]
    shaped = taps.reshape(channels, side, side, channels)
    out_rows = jnp.arange(SUB)[:, None, None]
    in_rows = jnp.arange(SLAB)[None, :, None]
    offsets = ((jnp.arange(side) - side // 2) * dilation)[None, None, :]
    hit = (in_rows == out_rows + HALO + offsets).astype(taps.dtype)
    full = jnp.einsum("oabc,rsa->orbcs", shaped, hit, preferred_element_type=jnp.float32)
    return full.reshape(channels * SUB, side * channels * SLAB).astype(taps.dtype)


def conv_kernel(u_ref, near_ref, far_ref, mix_ref, bias_ref, out_ref, *, first):
    channels, _, cols = out_ref.shape
    start = pl.multiple_of((pl.program_id(0) + first) * GROUP, GROUP)
    rows = u_ref[:, pl.ds(start, 2 * GROUP), :]
    bias = bias_ref[...]
    for sub in range(GROUP // SUB):
        slab = rows[:, sub * SUB : sub * SUB + SLAB, :].reshape(channels * SLAB, rows.shape[2])
        shifted = {d: slab[:, HALO + d : HALO + d + cols] for d in (-4, -2, -1, 0, 1, 2, 4)}
        near = jnp.dot(
            near_ref[...],
            jnp.concatenate([shifted[d] for d in (-1, 0, 1)], axis=0),
            preferred_element_type=jnp.float32,
        )
        far = jnp.dot(
            far_ref[...],
            jnp.concatenate([shifted[d] for d in (-4, -2, 0, 2, 4)], axis=0),
            preferred_element_type=jnp.float32,
        )
        total = mix_ref[1] * near + mix_ref[2] * far + bias
        out_ref[:, sub * SUB : (sub + 1) * SUB, :] = total.reshape(channels, SUB, cols)


def conv_call(padded, near, far, mixture, bias, rows, cols, first, count):
    channels = padded.shape[0]
    depth = near.shape[1] + far.shape[1]
    vmem = pl.BlockSpec(memory_space=pltpu.VMEM)
    return pl.pallas_call(
        lambda *refs: conv_kernel(*refs, first=first),
        grid=(count,),
        name="conv",
        out_shape=jax.ShapeDtypeStruct((channels, count * GROUP, cols), jnp.float32),
        in_specs=[vmem, vmem, vmem, pl.BlockSpec(memory_space=pltpu.SMEM), vmem],
        out_specs=pl.BlockSpec((channels, GROUP, cols), lambda i: (0, i, 0)),
        cost_estimate=pl.CostEstimate(
            flops=2 * channels * count * GROUP * cols * depth,
            bytes_accessed=channels * count * GROUP * cols * 6,
            transcendentals=0,
        ),
    )(padded, near, far, mixture, bias)


def split_bf16(value):
    high = value.astype(jnp.bfloat16)
    low = (value - high.astype(jnp.float32)).astype(jnp.bfloat16)
    return high, low


def finish_kernel(upper_ref, lower_ref, rows_ref, table_ref, *rest, halves):
    channels, _, cols = upper_ref.shape
    lines = rows_ref[...].reshape(channels * GROUP, rows_ref.shape[2])
    lines_high, lines_low = split_bf16(lines)
    table_high, table_low = split_bf16(table_ref[...])
    spectral = jnp.dot(
        jnp.concatenate([lines_high, lines_low, lines_high], axis=1),
        jnp.concatenate([table_high, table_high, table_low], axis=0),
        preferred_element_type=jnp.float32,
    )
    in_upper = pl.program_id(0) < halves
    conv = jnp.where(in_upper, upper_ref[...], lower_ref[...]).reshape(channels * GROUP, cols)
    value = conv + spectral
    out = (value * 0.5 * (1.0 + lax.erf(value * (0.5**0.5)))).astype(jnp.bfloat16)
    if len(rest) == 3:
        forward_ref, out_ref, lines_ref = rest
        sums = jnp.dot(out, forward_ref[...], preferred_element_type=jnp.float32)
        lines_ref[...] = sums.reshape(lines_ref.shape)
    else:
        (out_ref,) = rest
    out_ref[...] = out.reshape(out_ref.shape)


def finish_call(upper, lower, rows, table, forward):
    channels, upper_rows, cols = upper.shape
    halves = upper_rows // GROUP
    groups = halves + lower.shape[1] // GROUP
    width = rows.shape[2]
    vmem = pl.BlockSpec(memory_space=pltpu.VMEM)
    in_specs = [
        pl.BlockSpec((channels, GROUP, cols), lambda i: (0, jnp.minimum(i, halves - 1), 0)),
        pl.BlockSpec((channels, GROUP, cols), lambda i: (0, jnp.maximum(i - halves, 0), 0)),
        pl.BlockSpec((channels, GROUP, width), lambda i: (0, i, 0)),
        vmem,
    ]
    operands = [upper, lower, rows, table]
    shapes = [jax.ShapeDtypeStruct((channels, groups * GROUP, cols), jnp.bfloat16)]
    out_specs = [pl.BlockSpec((channels, GROUP, cols), lambda i: (0, i, 0))]
    if forward is not None:
        in_specs.append(vmem)
        operands.append(forward)
        shapes.append(jax.ShapeDtypeStruct((channels, groups * GROUP, width), jnp.float32))
        out_specs.append(pl.BlockSpec((channels, GROUP, width), lambda i: (0, i, 0)))
    results = pl.pallas_call(
        lambda *refs: finish_kernel(*refs, halves=halves),
        grid=(groups,),
        name="finish",
        out_shape=shapes,
        in_specs=in_specs,
        out_specs=out_specs,
        cost_estimate=pl.CostEstimate(
            flops=2 * channels * groups * GROUP * cols * 4 * width,
            bytes_accessed=channels * groups * GROUP * cols * 6,
            transcendentals=channels * groups * GROUP * cols,
        ),
    )(*operands)
    return results if forward is not None else (results[0], None)


def solution(mesh):
    def on_device(grid_field, spectral_weight, conv_near, conv_far, mix_logits, channel_bias):
        _, channels, local_rows, local_cols = grid_field.shape
        layers = spectral_weight.shape[0]
        share = spectral_weight.shape[-1]
        devices = lax.axis_size("gx") * lax.axis_size("gy")
        cells_x = local_rows * lax.axis_size("gx")
        cells_y = local_cols * lax.axis_size("gy")
        modes = share * devices
        modes_y = 32
        modes_x = modes // modes_y
        row_modes, col_modes = mode_numbers(modes_x, modes_y, cells_x)
        row_at = lax.axis_index("gx") * local_rows + jnp.arange(local_rows, dtype=jnp.int32)
        col_at = lax.axis_index("gy") * local_cols + jnp.arange(local_cols, dtype=jnp.int32)
        row_phase = (row_at[:, None] * row_modes[None, :] % cells_x).astype(jnp.float32) * (
            full_turn / cells_x
        )
        row_table = jnp.concatenate([jnp.cos(row_phase), jnp.sin(row_phase)], axis=1)
        col_phase = (col_at[:, None] * col_modes[None, :] % cells_y).astype(jnp.float32) * (
            full_turn / cells_y
        )
        col_table = jnp.concatenate([jnp.cos(col_phase), -jnp.sin(col_phase)], axis=1)
        forward = col_table.astype(jnp.bfloat16)
        col_weight = jnp.where(col_modes == 0, 1.0, 2.0).astype(jnp.float32) / (cells_x * cells_y)
        inverse = (col_table * jnp.concatenate([col_weight, col_weight])[None, :]).T
        exponents = jnp.exp(mix_logits)
        mixtures = exponents / jnp.sum(exponents, axis=1, keepdims=True)

        field = grid_field[0]
        lines = jnp.dot(
            field.reshape(channels * local_rows, local_cols),
            forward,
            preferred_element_type=jnp.float32,
        ).reshape(channels, local_rows, 2 * modes_y)
        groups = local_rows // GROUP
        upper_groups = (groups + 1) // 2
        for layer in range(layers):
            near = slab_weights(conv_near[layer], 1, 3)
            far = slab_weights(conv_far[layer], 2, 5)
            bias = jnp.repeat(channel_bias[layer], SUB)[:, None]
            padded = padded_field(field)

            def conv(near, first, count):
                return conv_call(
                    padded, near, far, mixtures[layer], bias, local_rows, local_cols, first, count
                )

            both = jnp.einsum("xj,cxk->jck", row_table, lines, precision=highest)
            cosine, sine = both[:modes_x], both[modes_x:]
            real = cosine[..., :modes_y] + sine[..., modes_y:]
            imaginary = cosine[..., modes_y:] - sine[..., :modes_y]
            partial = jnp.stack([real, imaginary])
            by_owner = partial.transpose(0, 2, 1, 3).reshape(2, channels, devices, share)
            by_owner = by_owner.transpose(2, 0, 1, 3)
            own = lax.psum_scatter(by_owner, ("gx", "gy"), scatter_dimension=0, tiled=True)[0]
            weight = spectral_weight[layer]
            own_real, own_imaginary = own[0][:, None, :], own[1][:, None, :]
            mixed_real = jnp.sum(weight[0] * own_real - weight[1] * own_imaginary, axis=0)
            mixed_imaginary = jnp.sum(weight[0] * own_imaginary + weight[1] * own_real, axis=0)
            own_block = jnp.stack([mixed_real, mixed_imaginary])[None] * mixtures[layer, 0]
            own_block, near_lower = lax.optimization_barrier((own_block, near))
            gathered = lax.all_gather(own_block, ("gx", "gy"), axis=0, tiled=True)
            full = gathered.transpose(1, 2, 0, 3).reshape(2, channels, modes_x, modes_y)
            spread = jnp.concatenate(
                [
                    jnp.concatenate([full[0], full[1]], axis=2),
                    jnp.concatenate([-full[1], full[0]], axis=2),
                ],
                axis=1,
            )
            upper = conv(near, 0, upper_groups)
            lower = conv(near_lower, upper_groups, groups - upper_groups)
            rows = jnp.einsum("xj,cjk->cxk", row_table, spread, precision=highest)
            field, lines = finish_call(
                upper, lower, rows, inverse, forward if layer + 1 < layers else None
            )
        return field[None]

    in_specs = (
        P(None, None, "gx", "gy"),
        P(None, None, None, None, ("gx", "gy")),
        P(),
        P(),
        P(),
        P(),
    )
    return jax.shard_map(
        on_device,
        mesh=mesh,
        in_specs=in_specs,
        out_specs=P(None, None, "gx", "gy"),
        check_vma=False,
    )
```

```python
import math

import jax
import jax.numpy as jnp
from jax import lax
from jax.experimental import pallas as pl
from jax.experimental.pallas import tpu as pltpu
from jax.sharding import PartitionSpec as P

full_turn = 2.0 * math.pi
highest = lax.Precision.HIGHEST
HALO = 4
GROUP = 16
SUB = 8
SLAB = SUB + 2 * HALO


def padded_field(value):
    for axis, dim in (("gx", 1), ("gy", 2)):
        size, length = (lax.axis_size(axis), value.shape[dim])
        up = [(i, (i + 1) % size) for i in range(size)]
        down = [(j, i) for i, j in up]
        last = lax.slice_in_dim(value, length - HALO, length, axis=dim)
        first = lax.slice_in_dim(value, 0, HALO, axis=dim)
        before = lax.ppermute(last, axis, up)
        after = lax.ppermute(first, axis, down)
        pieces = [before, value, after]
        if dim == 1:
            tail = value.shape[:1] + (GROUP - 2 * HALO,) + value.shape[2:]
            pieces.append(jnp.zeros(tail, value.dtype))
        value = jnp.concatenate(pieces, axis=dim)
    return value


def mode_numbers(modes_x, modes_y, cells_x):
    half = modes_x // 2
    lower = jnp.arange(half, dtype=jnp.int32)
    return jnp.concatenate([lower, lower + (cells_x - half)]), jnp.arange(modes_y, dtype=jnp.int32)


def slab_weights(taps, dilation, side):
    channels = taps.shape[0]
    lane = jnp.arange(channels * SLAB)
    spread = (lane[None, :] // SLAB == jnp.arange(channels)[:, None]).astype(taps.dtype)
    wide = jnp.dot(taps.reshape(-1, channels), spread, preferred_element_type=jnp.float32)
    wide = wide.reshape(channels, side, side, 1, channels * SLAB)
    reach = (lane % SLAB)[None, :] - HALO - jnp.arange(SUB)[:, None]
    columns = [
        sum(
            jnp.where(reach == (row - side // 2) * dilation, wide[:, row, column], 0.0)
            for row in range(side)
        )
        for column in range(side)
    ]
    full = jnp.concatenate(columns, axis=-1).astype(taps.dtype)
    return full.reshape(channels * SUB, side * channels * SLAB)


def conv_kernel(u_ref, near_ref, far_ref, mix_ref, bias_ref, out_ref, *, first):
    channels, _, cols = out_ref.shape
    start = pl.multiple_of((pl.program_id(0) + first) * GROUP, GROUP)
    rows = u_ref[:, pl.ds(start, 2 * GROUP), :]
    bias = bias_ref[...]
    for sub in range(GROUP // SUB):
        slab = rows[:, sub * SUB : sub * SUB + SLAB, :].reshape(channels * SLAB, rows.shape[2])
        shifted = {d: slab[:, HALO + d : HALO + d + cols] for d in (-4, -2, -1, 0, 1, 2, 4)}
        near = jnp.dot(
            near_ref[...],
            jnp.concatenate([shifted[d] for d in (-1, 0, 1)], axis=0),
            preferred_element_type=jnp.float32,
        )
        far = jnp.dot(
            far_ref[...],
            jnp.concatenate([shifted[d] for d in (-4, -2, 0, 2, 4)], axis=0),
            preferred_element_type=jnp.float32,
        )
        total = mix_ref[1] * near + mix_ref[2] * far + bias
        out_ref[:, sub * SUB : (sub + 1) * SUB, :] = total.reshape(channels, SUB, cols)


def conv_call(padded, near, far, mixture, bias, rows, cols, first, count):
    channels = padded.shape[0]
    depth = near.shape[1] + far.shape[1]
    vmem = pl.BlockSpec(memory_space=pltpu.VMEM)
    return pl.pallas_call(
        lambda *refs: conv_kernel(*refs, first=first),
        grid=(count,),
        name="conv",
        out_shape=jax.ShapeDtypeStruct((channels, count * GROUP, cols), jnp.float32),
        in_specs=[vmem, vmem, vmem, pl.BlockSpec(memory_space=pltpu.SMEM), vmem],
        out_specs=pl.BlockSpec((channels, GROUP, cols), lambda i: (0, i, 0)),
        cost_estimate=pl.CostEstimate(
            flops=2 * channels * count * GROUP * cols * depth,
            bytes_accessed=channels * count * GROUP * cols * 6,
            transcendentals=0,
        ),
    )(padded, near, far, mixture, bias)


def split_bf16(value):
    high = value.astype(jnp.bfloat16)
    low = (value - high.astype(jnp.float32)).astype(jnp.bfloat16)
    return high, low


def finish_kernel(upper_ref, lower_ref, rows_ref, table_ref, *rest, halves):
    channels, _, cols = upper_ref.shape
    lines = rows_ref[...].reshape(channels * GROUP, rows_ref.shape[2])
    lines_high, lines_low = split_bf16(lines)
    table_high, table_low = split_bf16(table_ref[...])
    spectral = jnp.dot(
        jnp.concatenate([lines_high, lines_low, lines_high], axis=1),
        jnp.concatenate([table_high, table_high, table_low], axis=0),
        preferred_element_type=jnp.float32,
    )
    in_upper = pl.program_id(0) < halves
    conv = jnp.where(in_upper, upper_ref[...], lower_ref[...]).reshape(channels * GROUP, cols)
    value = conv + spectral
    out = (value * 0.5 * (1.0 + lax.erf(value * (0.5**0.5)))).astype(jnp.bfloat16)
    if len(rest) == 3:
        forward_ref, out_ref, lines_ref = rest
        sums = jnp.dot(out, forward_ref[...], preferred_element_type=jnp.float32)
        lines_ref[...] = sums.reshape(lines_ref.shape)
    else:
        (out_ref,) = rest
    out_ref[...] = out.reshape(out_ref.shape)


def finish_call(upper, lower, rows, table, forward):
    channels, upper_rows, cols = upper.shape
    halves = upper_rows // GROUP
    groups = halves + lower.shape[1] // GROUP
    width = rows.shape[2]
    vmem = pl.BlockSpec(memory_space=pltpu.VMEM)
    in_specs = [
        pl.BlockSpec((channels, GROUP, cols), lambda i: (0, jnp.minimum(i, halves - 1), 0)),
        pl.BlockSpec((channels, GROUP, cols), lambda i: (0, jnp.maximum(i - halves, 0), 0)),
        pl.BlockSpec((channels, GROUP, width), lambda i: (0, i, 0)),
        vmem,
    ]
    operands = [upper, lower, rows, table]
    shapes = [jax.ShapeDtypeStruct((channels, groups * GROUP, cols), jnp.bfloat16)]
    out_specs = [pl.BlockSpec((channels, GROUP, cols), lambda i: (0, i, 0))]
    if forward is not None:
        in_specs.append(vmem)
        operands.append(forward)
        shapes.append(jax.ShapeDtypeStruct((channels, groups * GROUP, width), jnp.float32))
        out_specs.append(pl.BlockSpec((channels, GROUP, width), lambda i: (0, i, 0)))
    results = pl.pallas_call(
        lambda *refs: finish_kernel(*refs, halves=halves),
        grid=(groups,),
        name="finish",
        out_shape=shapes,
        in_specs=in_specs,
        out_specs=out_specs,
        cost_estimate=pl.CostEstimate(
            flops=2 * channels * groups * GROUP * cols * 4 * width,
            bytes_accessed=channels * groups * GROUP * cols * 6,
            transcendentals=channels * groups * GROUP * cols,
        ),
    )(*operands)
    return results if forward is not None else (results[0], None)


def solution(mesh):
    def on_device(grid_field, spectral_weight, conv_near, conv_far, mix_logits, channel_bias):
        _, channels, local_rows, local_cols = grid_field.shape
        layers = spectral_weight.shape[0]
        share = spectral_weight.shape[-1]
        devices = lax.axis_size("gx") * lax.axis_size("gy")
        cells_x = local_rows * lax.axis_size("gx")
        cells_y = local_cols * lax.axis_size("gy")
        modes = share * devices
        modes_y = 32
        modes_x = modes // modes_y
        row_modes, col_modes = mode_numbers(modes_x, modes_y, cells_x)
        row_at = lax.axis_index("gx") * local_rows + jnp.arange(local_rows, dtype=jnp.int32)
        col_at = lax.axis_index("gy") * local_cols + jnp.arange(local_cols, dtype=jnp.int32)
        row_phase = (row_at[:, None] * row_modes[None, :] % cells_x).astype(jnp.float32) * (
            full_turn / cells_x
        )
        row_table = jnp.concatenate([jnp.cos(row_phase), jnp.sin(row_phase)], axis=1)
        col_phase = (col_at[:, None] * col_modes[None, :] % cells_y).astype(jnp.float32) * (
            full_turn / cells_y
        )
        col_table = jnp.concatenate([jnp.cos(col_phase), -jnp.sin(col_phase)], axis=1)
        forward = col_table.astype(jnp.bfloat16)
        col_weight = jnp.where(col_modes == 0, 1.0, 2.0).astype(jnp.float32) / (cells_x * cells_y)
        inverse = (col_table * jnp.concatenate([col_weight, col_weight])[None, :]).T
        exponents = jnp.exp(mix_logits)
        mixtures = exponents / jnp.sum(exponents, axis=1, keepdims=True)

        field = grid_field[0]
        lines = jnp.dot(
            field.reshape(channels * local_rows, local_cols),
            forward,
            preferred_element_type=jnp.float32,
        ).reshape(channels, local_rows, 2 * modes_y)
        groups = local_rows // GROUP
        upper_groups = (groups + 1) // 2
        for layer in range(layers):
            near = slab_weights(conv_near[layer], 1, 3)
            far = slab_weights(conv_far[layer], 2, 5)
            bias = jnp.repeat(channel_bias[layer], SUB)[:, None]
            padded = padded_field(field)

            def conv(near, first, count):
                return conv_call(
                    padded, near, far, mixtures[layer], bias, local_rows, local_cols, first, count
                )

            both = jnp.einsum("xj,cxk->jck", row_table, lines, precision=highest)
            cosine, sine = both[:modes_x], both[modes_x:]
            real = cosine[..., :modes_y] + sine[..., modes_y:]
            imaginary = cosine[..., modes_y:] - sine[..., :modes_y]
            partial = jnp.stack([real, imaginary])
            by_owner = partial.transpose(0, 2, 1, 3).reshape(2, channels, devices, share)
            by_owner = by_owner.transpose(2, 0, 1, 3)
            parts = lax.all_to_all(by_owner, ("gx", "gy"), 0, 0, tiled=True)
            own = jnp.sum(parts, axis=0)
            weight = spectral_weight[layer]
            own_real, own_imaginary = own[0][:, None, :], own[1][:, None, :]
            mixed_real = jnp.sum(weight[0] * own_real - weight[1] * own_imaginary, axis=0)
            mixed_imaginary = jnp.sum(weight[0] * own_imaginary + weight[1] * own_real, axis=0)
            own_block = jnp.stack([mixed_real, mixed_imaginary])[None] * mixtures[layer, 0]
            own_block, near_lower = lax.optimization_barrier((own_block, near))
            copies = jnp.broadcast_to(own_block, (devices,) + own_block.shape[1:])
            gathered = lax.all_to_all(copies, ("gx", "gy"), 0, 0, tiled=True)
            full = gathered.transpose(1, 2, 0, 3).reshape(2, channels, modes_x, modes_y)
            spread = jnp.concatenate(
                [
                    jnp.concatenate([full[0], full[1]], axis=2),
                    jnp.concatenate([-full[1], full[0]], axis=2),
                ],
                axis=1,
            )
            upper = conv(near, 0, upper_groups)
            lower = conv(near_lower, upper_groups, groups - upper_groups)
            rows = jnp.einsum("xj,cjk->cxk", row_table, spread, precision=highest)
            field, lines = finish_call(
                upper, lower, rows, inverse, forward if layer + 1 < layers else None
            )
        return field[None]

    in_specs = (
        P(None, None, "gx", "gy"),
        P(None, None, None, None, ("gx", "gy")),
        P(),
        P(),
        P(),
        P(),
    )
    return jax.shard_map(
        on_device,
        mesh=mesh,
        in_specs=in_specs,
        out_specs=P(None, None, "gx", "gy"),
        check_vma=False,
    )
```
